32 devices in a mesh: group: 2 (over y), ep: 4 (over x, core), tp: 4 (over z).
Axes of the slice: x: 2, y: 2, z: 4, core: 2. Of those that a mesh axis runs over, the one named last changes fastest.
Arguments:
- tokens: bfloat16 [192, 3072], P(('group', 'ep', 'tp')), parts along dimension 0, may hold values from -6 to 6
- experts: int32 [192, 2], P(('group', 'ep', 'tp')), parts along dimension 0, may hold values from 0 to 3, as said below
- replicas: int32 [192, 2], P(('group', 'ep', 'tp')), parts along dimension 0, may hold values from 0 to 2, as said below
- gates: float32 [192, 2], P(('group', 'ep', 'tp')), parts along dimension 0, may hold values from 0.1 to 1
- w_gate: bfloat16 [16, 3072, 4096], P('ep', None, 'tp'), may hold values from -0.109375 to 0.109375
- w_up: bfloat16 [16, 3072, 4096], P('ep', None, 'tp'), may hold values from -0.109375 to 0.109375
- w_down: bfloat16 [16, 4096, 3072], P('ep', 'tp'), may hold values from -0.0625 to 0.0625
Outputs:
- moe_output: bfloat16 [192, 3072], P(('group', 'ep', 'tp')), parts along dimension 0
The draws below stay inside these ranges and needn't reach their ends.
There are 2 independent parts, one for each index of `group`. The reference program is written for one: setup_inputs(seed, part) draws one part's arguments, and reference() takes and returns one part's arrays. A program takes and returns all parts, laid end to end along the dimension named above; an argument that names none is the same for every part. Nothing has to cross between parts.
Inputs may be any that keep to these rules, and one draw needn't show every extreme that they name: The two experts of a row differ. `replicas`: a replica above 0 stands only beside an expert below 2; the picks of the rows of one device name one instance at most 2 times, exactly 2 times for some instance on every device; the picks of the rows of all devices with one index of tp name one instance at most 8 times, exactly 8 times for some instance.
All inputs are finite; a program needn't handle non-finite values.
Results may differ from the reference program's by a relative error of at most 0.018.
Values may be sent and summed in bfloat16 or wider, within the bound.
No kernel may reach another device: no remote copies, remote signals or barrier semaphores. Data moves between devices by JAX's collectives and lax.ppermute only.
A program may use at most 128 MiB of HBM per device.

```python
import jax
import jax.numpy as jnp
from jax import lax

D = 3072
EXPERTS = 4
FF = 8192
SPLIT = 2
TOK_DEV = 6
FF_TP = 1024
RECV = 8
INST = 8
PIECES = 16
TOKENS = 96
N_EP = 4
N_TP = 4


def routed_instances(key):
    base_key = jax.random.fold_in(key, 11)
    key_col, key_other, key_rows, key_flip = jax.random.split(base_key, 4)
    pair_count = EXPERTS
    column_type = jax.random.randint(key_col, (N_TP,), 0, pair_count)
    full_type = jnp.broadcast_to(column_type[None, :], (N_EP, N_TP))
    other_type = (full_type + jax.random.randint(key_other, (N_EP, N_TP), 1, pair_count)) % pair_count
    kinds = jnp.arange(pair_count)[None, None, :]
    unused = (kinds != full_type[:, :, None]) & (kinds != other_type[:, :, None])
    low_rest = jnp.min(jnp.where(unused, kinds, 99), axis=2)
    high_rest = jnp.max(jnp.where(unused, kinds, -1), axis=2)
    row_types = jnp.stack([full_type, full_type, other_type, other_type, low_rest, high_rest], axis=-1)
    row_order = jax.vmap(lambda sub_key: jax.random.permutation(sub_key, TOK_DEV))(jax.random.split(key_rows, N_EP * N_TP)).reshape(N_EP, N_TP, TOK_DEV)
    row_types = jnp.take_along_axis(row_types, row_order, axis=2)
    flip_bit = jax.random.randint(key_flip, (N_EP, N_TP, TOK_DEV), 0, 2)
    first_pick = row_types + EXPERTS * flip_bit
    second = row_types + EXPERTS * (1 - flip_bit)
    both_picks = jnp.stack([first_pick, second], axis=-1)
    return both_picks.reshape(TOKENS, 2).astype(jnp.int32)


def draw_experts(key, part):
    picked = routed_instances(key)
    half_count = EXPERTS // 2
    return jnp.where(picked < EXPERTS, picked, (picked - EXPERTS + 1) % half_count).astype(jnp.int32)


def draw_replicas(key, part):
    picked = routed_instances(key)
    half_count = EXPERTS // 2
    return jnp.where(picked < EXPERTS, 0, 1 + (picked - EXPERTS) // half_count).astype(jnp.int32)


def level_of(rng, extent, cuts, least, largest):
    loudness = 1.0
    for position, shards_of in cuts:
        heights = jax.random.uniform(jax.random.fold_in(jax.random.fold_in(rng, 6), position), (shards_of,), jnp.float32, least / len(cuts), largest / len(cuts))
        loudness = loudness * jnp.repeat(jnp.exp(heights), extent[position] // shards_of).reshape((-1,) + (1,) * (len(extent) - 1 - position))
    return loudness


def noise(stream_key, shape, deviation, limit, cuts=(), held_as=jnp.bfloat16):
    result = jax.random.normal(stream_key, shape, jnp.float32) * deviation
    if len(cuts) > 0:
        result = level_of(stream_key, shape, cuts, -0.22, 0.18) * result
    return jnp.clip(result, min=-limit, max=limit).astype(held_as)


def setup_inputs(seed: int = 0, part: int = 0) -> dict:
    key_of = jax.random.split(jax.random.key(seed), 8)
    own_keys = jax.random.split(jax.random.fold_in(key_of[7], part), 8)
    return {
        "tokens": noise(own_keys[0], (TOKENS, D), 1.0, 6.0, ((0, 16),)),
        "experts": draw_experts(jax.random.fold_in(jax.random.fold_in(key_of[7], part), 71), part),
        "replicas": draw_replicas(jax.random.fold_in(jax.random.fold_in(key_of[7], part), 71), part),
        "gates": jnp.clip(0.1 + 0.9 * jax.random.uniform(own_keys[3], (TOKENS, 2), jnp.float32) ** level_of(own_keys[3], (TOKENS, 2), ((0, 16),), -0.2, 0.2), 0.1, 1.0),
        "w_gate": noise(key_of[4], (PIECES, D, FF // SPLIT), D ** -0.5, 0.109375, ((0, 4), (2, 4))),
        "w_up": noise(key_of[5], (PIECES, D, FF // SPLIT), D ** -0.5, 0.109375, ((0, 4), (2, 4))),
        "w_down": noise(key_of[6], (PIECES, FF // SPLIT, D), FF ** -0.5, 0.0625, ((0, 4), (1, 4))),
    }


def reference(tokens, experts, replicas, gates, w_gate, w_up, w_down):
    hot_count = EXPERTS // 2
    instance = jnp.where(replicas == 0, experts, EXPERTS + (replicas - 1) * hot_count + (experts - 1) % hot_count)
    flat_inst = instance.reshape(-1).astype(jnp.int32)
    pick_total = flat_inst.shape[0]
    most_rows = RECV * N_TP

    def per_instance(inst_id):
        matched = flat_inst == inst_id
        pick_index = jnp.nonzero(matched, size=most_rows, fill_value=0)[0].astype(jnp.int32)
        is_valid = jnp.arange(most_rows) < jnp.sum(matched.astype(jnp.int32))
        row_data = tokens[pick_index // 2]
        total = jnp.zeros((most_rows, D), jnp.float32)
        for half in range(SPLIT):
            piece_id = inst_id * SPLIT + half
            gate_act = jnp.dot(row_data, w_gate[piece_id], preferred_element_type=jnp.float32)
            up_act = jnp.dot(row_data, w_up[piece_id], preferred_element_type=jnp.float32)
            hidden = (jax.nn.silu(gate_act) * up_act).astype(jnp.bfloat16)
            blocks = hidden.reshape(most_rows, N_TP, FF_TP).astype(jnp.float32)
            down_blocks = w_down[piece_id].reshape(N_TP, FF_TP, D).astype(jnp.float32)
            partial_value = jnp.einsum("mtf,tfd->tmd", blocks, down_blocks)
            partial_value = lax.optimization_barrier(partial_value.astype(jnp.bfloat16))
            piece_out = jnp.sum(partial_value.astype(jnp.float32), axis=0).astype(jnp.bfloat16)
            total = total + piece_out.astype(jnp.float32)
        return pick_index, total, is_valid

    indices, outputs, valids = lax.map(per_instance, jnp.arange(INST, dtype=jnp.int32))
    contrib = jnp.where(valids.reshape(-1, 1), outputs.reshape(-1, D), jnp.float32(0.0))
    pick_out = jnp.zeros((pick_total, D), jnp.float32).at[indices.reshape(-1)].add(contrib)
    mixed = jnp.sum(pick_out.reshape(TOKENS, 2, D) * gates[:, :, None], axis=1)
    return mixed.astype(jnp.bfloat16)
```

```python
import functools

import jax
import jax.numpy as jnp
from jax import lax
from jax.experimental import pallas as pl
from jax.experimental.pallas import tpu as pltpu
from jax.sharding import PartitionSpec as P

SPLIT = 2
LANES = 128
META = 2


def partner(count, step):
    if count & (count - 1) == 0:
        return [(i, i ^ step) for i in range(count)]
    return [(i, (i + step) % count) for i in range(count)]


def back(count, step):
    return [(dst, src) for src, dst in partner(count, step)]


def stages(count, direct):
    if direct or count & (count - 1) != 0:
        return [list(range(1, count))]
    found, bit = [], count // 2
    while bit >= 1:
        found.append([bit])
        bit //= 2
    return found


def gather(rows, axis, direct):
    count = lax.axis_size(axis)
    for steps in stages(count, direct):
        arrived = [lax.ppermute(rows, axis, partner(count, step)) for step in steps]
        rows = jnp.concatenate([rows] + arrived, axis=0)
    return rows


def scatter_sum(rows, axis, direct):
    count = lax.axis_size(axis)
    for steps in reversed(stages(count, direct)):
        parts = jnp.split(rows, len(steps) + 1, axis=0)
        arrived = [
            lax.ppermute(part, axis, back(count, step)) for part, step in zip(parts[1:], steps)
        ]
        total = parts[0].astype(jnp.float32)
        for part in arrived:
            total = total + part.astype(jnp.float32)
        rows = total.astype(jnp.bfloat16)
    return rows


def pack_kernel(inst_count, tokens, experts, replicas, gates, out, wide):
    rows_dev, features = tokens.shape
    expert_count = inst_count // 2
    hot_count = expert_count // 2
    wide[...] = jnp.zeros_like(wide)
    wide[:rows_dev, :] = tokens[...].astype(jnp.float32)
    picked, copy = experts[...], replicas[...]
    turn = jnp.zeros_like(picked)
    for e in range(expert_count):
        turn = jnp.where(picked == e, (e - 1) % hot_count, turn)
    instance = jnp.where(copy == 0, picked, expert_count + (copy - 1) * hot_count + turn)
    for i in range(inst_count):
        weight = jnp.sum(jnp.where(instance == i, gates[...], 0.0), axis=0, keepdims=True)
        high = weight.astype(jnp.bfloat16).astype(jnp.float32)
        low = (weight - high).astype(jnp.bfloat16).astype(jnp.float32)
        lanes = slice(i * LANES, i * LANES + rows_dev)
        wide[rows_dev : rows_dev + 1, lanes] = high
        wide[rows_dev + 1 : rows_dev + 2, lanes] = low
    out[...] = wide[...].astype(jnp.bfloat16)


def pack(tokens, experts, replicas, gates, inst_count):
    rows_dev, features = tokens.shape
    block = -(-(rows_dev + META) // 8) * 8
    return pl.pallas_call(
        functools.partial(pack_kernel, inst_count),
        out_shape=jax.ShapeDtypeStruct((block, features), jnp.bfloat16),
        scratch_shapes=[pltpu.VMEM((block, features), jnp.float32)],
    )(tokens, experts.T, replicas.T, gates.T)


def expert_kernel(block, rows_dev, first_ref, x, w_gate, w_up, w_down, out, total):
    piece, part = pl.program_id(1), pl.program_id(2)
    tile = x.shape[0]
    begin = (piece == 0) & (part == 0)
    instance = (first_ref[0] + piece) // SPLIT
    lanes = pl.ds(pl.multiple_of(instance * LANES, LANES), LANES)
    slab = x[:, lanes].astype(jnp.float32).reshape(tile // block, block, LANES)
    weight = slab[:, rows_dev : rows_dev + 1, :] + slab[:, rows_dev + 1 : rows_dev + 2, :]
    shape = (tile // block, block, LANES)
    row = lax.broadcasted_iota(jnp.int32, shape, 1)
    lane = lax.broadcasted_iota(jnp.int32, shape, 2)
    own = jnp.where((row == lane) & (row < rows_dev), jnp.broadcast_to(weight, shape), 0.0)
    coef = jnp.sum(own, axis=2, keepdims=True).reshape(tile, 1)
    gate_act = jnp.dot(x[...], w_gate[0], preferred_element_type=jnp.float32)
    up_act = jnp.dot(x[...], w_up[0], preferred_element_type=jnp.float32)
    hidden = (gate_act / (1.0 + jnp.exp(-gate_act)) * up_act * coef).astype(jnp.bfloat16)
    share = jnp.dot(hidden, w_down[0], preferred_element_type=jnp.float32)

    @pl.when(begin)
    def _():
        total[...] = share

    @pl.when(jnp.logical_not(begin))
    def _():
        total[...] += share

    @pl.when((piece == pl.num_programs(1) - 1) & (part == pl.num_programs(2) - 1))
    def _():
        out[...] = total[...].astype(jnp.bfloat16)


def experts_of(x, first, w_gate, w_up, w_down, block, rows_dev):
    rows, features = x.shape
    pieces, _, hidden_dev = w_gate.shape
    width = min(512, hidden_dev)
    tile = min(rows, 128)
    return pl.pallas_call(
        functools.partial(expert_kernel, block, rows_dev),
        out_shape=jax.ShapeDtypeStruct((rows, features), jnp.bfloat16),
        grid_spec=pltpu.PrefetchScalarGridSpec(
            num_scalar_prefetch=1,
            grid=(rows // tile, pieces, hidden_dev // width),
            in_specs=[
                pl.BlockSpec((tile, features), lambda r, q, f, s: (r, 0)),
                pl.BlockSpec((1, features, width), lambda r, q, f, s: (q, 0, f)),
                pl.BlockSpec((1, features, width), lambda r, q, f, s: (q, 0, f)),
                pl.BlockSpec((1, width, features), lambda r, q, f, s: (q, f, 0)),
            ],
            out_specs=pl.BlockSpec((tile, features), lambda r, q, f, s: (r, 0)),
            scratch_shapes=[pltpu.VMEM((tile, features), jnp.float32)],
        ),
        compiler_params=pltpu.CompilerParams(vmem_limit_bytes=40 << 20),
    )(first, x, w_gate, w_up, w_down)


def on_device(tokens, experts, replicas, gates, w_gate, w_up, w_down):
    local_piece = w_gate.shape[0]
    inst_count = local_piece * lax.axis_size("ep") // SPLIT
    rows_dev = tokens.shape[0]
    direct = lax.axis_size("tp") <= 4
    block_rows = pack(tokens, experts, replicas, gates, inst_count)
    block = block_rows.shape[0]
    rows = gather(block_rows, "tp", direct)
    rows = gather(rows, "ep", False)
    first = (lax.axis_index("ep") * local_piece).astype(jnp.int32).reshape(1)
    share = experts_of(rows, first, w_gate, w_up, w_down, block, rows_dev)
    share = scatter_sum(share, "ep", False)
    share = scatter_sum(share, "tp", direct)
    return share[:rows_dev]


def solution(mesh):
    return jax.shard_map(
        on_device,
        mesh=mesh,
        in_specs=(
            P(("group", "ep", "tp"), None),
            P(("group", "ep", "tp"), None),
            P(("group", "ep", "tp"), None),
            P(("group", "ep", "tp"), None),
            P("ep", None, "tp"),
            P("ep", None, "tp"),
            P("ep", "tp", None),
        ),
        out_specs=P(("group", "ep", "tp"), None),
        check_vma=False,
    )
```

```python
import functools

import jax
import jax.numpy as jnp
from jax import lax
from jax.experimental import pallas as pl
from jax.experimental.pallas import tpu as pltpu
from jax.sharding import PartitionSpec as P

SPLIT = 2
LANES = 128
META = 2
WIDTH = 512
LOADS = (4, 4)
RING = [4, 2]


def partner(count, step):
    if count & (count - 1) == 0:
        return [(i, i ^ step) for i in range(count)]
    return [(i, (i + step) % count) for i in range(count)]


def back(count, step):
    return [(dst, src) for src, dst in partner(count, step)]


def stages(count, direct):
    if direct or count & (count - 1) != 0:
        return [list(range(1, count))]
    found, bit = [], count // 2
    while bit >= 1:
        found.append([bit])
        bit //= 2
    return found


def gather(rows, axis, direct):
    count = lax.axis_size(axis)
    for steps in stages(count, direct):
        arrived = []
        for step in steps:
            arrived.append(lax.ppermute(rows, axis, partner(count, step)))
        rows = jnp.concatenate([rows] + arrived, axis=0)
    return rows


def scatter_sum(rows, axis, direct):
    count = lax.axis_size(axis)
    for steps in reversed(stages(count, direct)):
        parts = jnp.split(rows, len(steps) + 1, axis=0)
        arrived = [
            lax.ppermute(part, axis, back(count, step)) for part, step in zip(parts[1:], steps)
        ]
        total = parts[0].astype(jnp.float32)
        for part in arrived:
            total = total + part.astype(jnp.float32)
        rows = total.astype(jnp.bfloat16)
    return rows


def pack_kernel(inst_count, tokens, experts, replicas, gates, out, wide):
    rows_dev, _ = tokens.shape
    expert_count = inst_count // 2
    hot_count = expert_count // 2
    wide[...] = jnp.zeros_like(wide)
    wide[:rows_dev, :] = tokens[...].astype(jnp.float32)
    picked, copy = experts[...], replicas[...]
    turn = jnp.zeros_like(picked)
    for e in range(expert_count):
        turn = jnp.where(picked == e, (e - 1) % hot_count, turn)
    instance = jnp.where(copy == 0, picked, expert_count + (copy - 1) * hot_count + turn)
    for i in range(inst_count):
        weight = jnp.sum(jnp.where(instance == i, gates[...], 0.0), axis=0, keepdims=True)
        high = weight.astype(jnp.bfloat16).astype(jnp.float32)
        low = (weight - high).astype(jnp.bfloat16).astype(jnp.float32)
        lanes = slice(i * LANES, i * LANES + rows_dev)
        wide[rows_dev : rows_dev + 1, lanes] = high
        wide[rows_dev + 1 : rows_dev + 2, lanes] = low
    out[...] = wide[...].astype(jnp.bfloat16)


def pack(tokens, experts, replicas, gates, inst_count):
    rows_dev, features = tokens.shape
    block = -(-(rows_dev + META) // 8) * 8
    return pl.pallas_call(
        functools.partial(pack_kernel, inst_count),
        out_shape=jax.ShapeDtypeStruct((block, features), jnp.bfloat16),
        scratch_shapes=[pltpu.VMEM((block, features), jnp.float32)],
        compiler_params=pltpu.CompilerParams(vmem_limit_bytes=2 << 20),
    )(tokens, experts.T, replicas.T, gates.T)


def coef_of(slab, block, rows_dev):
    tile = slab.shape[0]
    shape = (tile // block, block, LANES)
    slab = slab.astype(jnp.float32).reshape(shape)
    weight = slab[:, rows_dev : rows_dev + 1, :] + slab[:, rows_dev + 1 : rows_dev + 2, :]
    row = lax.broadcasted_iota(jnp.int32, shape, 1)
    lane = lax.broadcasted_iota(jnp.int32, shape, 2)
    own = jnp.where((row == lane) & (row < rows_dev), jnp.broadcast_to(weight, shape), 0.0)
    return jnp.sum(own, axis=2, keepdims=True).reshape(tile, 1)


class Plan:
    def __init__(self, w_gate):
        self.pieces, self.features, self.hidden = w_gate.shape
        self.width = min(WIDTH, self.hidden)
        self.parts = self.hidden // self.width
        self.jobs = self.pieces * self.parts
        self.units = 3 * self.jobs
        self.loads, begin = [], 0
        for count in LOADS:
            end = min(begin + count, self.units)
            self.loads.append(range(begin, end))
            begin = end
        self.ready = begin

    def shape(self, unit):
        if unit % 3 == 2:
            return (self.width, self.features)
        return (self.features, self.width)

    def source(self, weights, unit):
        job, kind = unit // 3, unit % 3
        piece, span = job // self.parts, pl.ds(job % self.parts * self.width, self.width)
        if kind == 2:
            return weights[2].at[piece, span, :]
        return weights[kind].at[piece, :, span]


def load_kernel(plan, units, *refs):
    weights, slots, sems = refs[:3], refs[4:-1], refs[-1]
    copies = [
        pltpu.make_async_copy(plan.source(weights, unit), slots[n], sems.at[n])
        for n, unit in enumerate(units)
    ]
    for copy in copies:
        copy.start()
    for copy in copies:
        copy.wait()


def load(plan, index, weights, after):
    units = plan.loads[index]
    if len(units) == 0:
        return []
    anywhere = pl.BlockSpec(memory_space=pltpu.HBM)
    inside = pl.BlockSpec(memory_space=pltpu.VMEM)
    moved = len(units) * plan.features * plan.width * 2
    found = pl.pallas_call(
        functools.partial(load_kernel, plan, units),
        out_shape=[pltpu.VMEM(plan.shape(unit), jnp.bfloat16) for unit in units],
        in_specs=[anywhere] * 3 + [pl.BlockSpec(memory_space=pl.ANY)],
        out_specs=[inside] * len(units),
        scratch_shapes=[pltpu.SemaphoreType.DMA((len(units),))],
        compiler_params=pltpu.CompilerParams(vmem_limit_bytes=1 << 20),
        cost_estimate=pl.CostEstimate(flops=0, bytes_accessed=moved, transcendentals=0),
    )(*weights, after)
    return list(found)


def expert_kernel(plan, block, rows_dev, x, w_gate, w_up, w_down, *refs):
    held, (out, total, wide, tall, sems) = refs[: plan.ready], refs[plan.ready :]
    weights, rings = (w_gate, w_up, w_down), (wide, tall)
    tile = total.shape[0]
    first = lax.axis_index("ep") * plan.pieces
    streams = [
        [u for u in range(plan.ready, plan.units) if u % 3 != 2],
        [u for u in range(plan.ready, plan.units) if u % 3 == 2],
    ]
    depth = [wide.shape[0], tall.shape[0]]
    place = {u: (s, n) for s, units in enumerate(streams) for n, u in enumerate(units)}

    def fetch(unit):
        s, n = place[unit]
        slot = n % depth[s]
        return pltpu.make_async_copy(plan.source(weights, unit), rings[s].at[slot], sems.at[s, slot])

    def use(unit):
        if unit < plan.ready:
            return held[unit]
        fetch(unit).wait()
        s, n = place[unit]
        return rings[s].at[n % depth[s]]

    def free(unit):
        if unit >= plan.ready:
            s, n = place[unit]
            if n + depth[s] < len(streams[s]):
                fetch(streams[s][n + depth[s]]).start()

    def per_tile(r, carry):
        rows = pl.ds(pl.multiple_of(r * tile, tile), tile)
        for unit in range(plan.ready, plan.units):
            s, n = place[unit]
            if n < depth[s]:
                fetch(unit).start()
        for job in range(plan.jobs):
            instance = (first + job // plan.parts) // SPLIT
            lanes = pl.ds(pl.multiple_of(instance * LANES, LANES), LANES)
            coef = coef_of(x[rows, lanes], block, rows_dev)
            gate_act = jnp.dot(x[rows, :], use(3 * job)[...], preferred_element_type=jnp.float32)
            free(3 * job)
            up_act = jnp.dot(x[rows, :], use(3 * job + 1)[...], preferred_element_type=jnp.float32)
            free(3 * job + 1)
            hidden = gate_act / (1.0 + jnp.exp(-gate_act)) * up_act * coef
            share = jnp.dot(
                hidden.astype(jnp.bfloat16),
                use(3 * job + 2)[...],
                preferred_element_type=jnp.float32,
            )
            free(3 * job + 2)
            if job > 0:
                share = total[...] + share
            if job < plan.jobs - 1:
                total[...] = share
            else:
                out[rows, :] = share.astype(jnp.bfloat16)
        return carry

    if x.shape[0] == tile:
        per_tile(0, 0)
    else:
        lax.fori_loop(0, x.shape[0] // tile, per_tile, 0)


def experts_of(plan, x, weights, held, block, rows_dev):
    rows, features = x.shape
    tile = min(rows, 128)
    anywhere = pl.BlockSpec(memory_space=pltpu.HBM)
    inside = pl.BlockSpec(memory_space=pltpu.VMEM)
    held = [pltpu.with_memory_space_constraint(unit, pltpu.VMEM) for unit in held]
    limit = 4 << 20
    depth = [1, 1]
    if plan.ready < plan.units:
        depth = RING
    limit += sum(depth) * plan.width * features * 2
    return pl.pallas_call(
        functools.partial(expert_kernel, plan, block, rows_dev),
        out_shape=jax.ShapeDtypeStruct((rows, features), jnp.bfloat16),
        in_specs=[inside] + [anywhere] * 3 + [inside] * len(held),
        out_specs=inside,
        scratch_shapes=[
            pltpu.VMEM((tile, features), jnp.float32),
            pltpu.VMEM((depth[0], features, plan.width), jnp.bfloat16),
            pltpu.VMEM((depth[1], plan.width, features), jnp.bfloat16),
            pltpu.SemaphoreType.DMA((2, max(depth))),
        ],
        compiler_params=pltpu.CompilerParams(vmem_limit_bytes=limit),
    )(x, *weights, *held)


def on_device(tokens, experts, replicas, gates, w_gate, w_up, w_down):
    plan = Plan(w_gate)
    weights = [pltpu.with_memory_space_constraint(w, pltpu.HBM) for w in (w_gate, w_up, w_down)]
    inst_count = plan.pieces * lax.axis_size("ep") // SPLIT
    rows_dev = tokens.shape[0]
    direct = lax.axis_size("tp") <= 4
    block_rows = pack(tokens, experts, replicas, gates, inst_count)
    block = block_rows.shape[0]
    held = load(plan, 0, weights, block_rows)
    rows = gather(block_rows, "tp", direct)
    held = held + load(plan, 1, weights, rows)
    rows = gather(rows, "ep", False)
    share = experts_of(plan, rows, weights, held, block, rows_dev)
    share = scatter_sum(share, "ep", False)
    share = scatter_sum(share, "tp", direct)
    return share[:rows_dev]


def solution(mesh):
    return jax.shard_map(
        on_device,
        mesh=mesh,
        in_specs=(
            P(("group", "ep", "tp"), None),
            P(("group", "ep", "tp"), None),
            P(("group", "ep", "tp"), None),
            P(("group", "ep", "tp"), None),
            P("ep", None, "tp"),
            P("ep", None, "tp"),
            P("ep", "tp", None),
        ),
        out_specs=P(("group", "ep", "tp"), None),
        check_vma=False,
    )
```
